1024 devices in a mesh: ctx: 32 (over x, z_lo), fsdp: 32 (over y, z_hi, core).
Axes of the slice: x: 4, y: 4, z: 32 (z_hi: 4, z_lo: 8; z = z_hi * 8 + z_lo), core: 2. Of those that a mesh axis runs over, the one named last changes fastest.
Arguments:
- tokens: bfloat16 [8192, 7168], P('ctx', 'fsdp'), may hold values from -6 to 6
- kv_down: bfloat16 [7168, 576], P('fsdp'), may hold values from -0.0625 to 0.0625
- norm_gain: float32 [512], replicated, may hold values from 0.1 to 1.9
- queries: bfloat16 [8192, 128, 576], P('ctx', 'fsdp'), may hold values from -102 to 102, as said below
Outputs:
- mixed: bfloat16 [8192, 128, 512], P('ctx', 'fsdp')
The draws below stay inside these ranges and needn't reach their ends.
Inputs may be any that keep to these rules, and one draw needn't show every extreme that they name: real-valued queries.
All inputs are finite; a program needn't handle non-finite values.
Results may differ from the reference program's by a relative error of at most 0.01225.
The reference program's roundings to bfloat16 on the way (of `key_rows` and `weights`) count: a program that leaves them out, or rounds other values in their place, can miss the bound.
Values may be sent and summed in bfloat16 or wider, within the bound.
No kernel may reach another device: no remote copies, remote signals or barrier semaphores. Data moves between devices by JAX's collectives and lax.ppermute only.
A program may use at most 32 MiB of HBM per device.

```python
import jax
import jax.numpy as jnp
from jax import lax

D = 7168
LATENT = 512
ROPE = 64
HEADS = 128
TOK_DEV = 256
REACH = 3
SEQ = 8192
N_CTX = 32


def draw_queries(key, part):
    shape = (SEQ, HEADS, LATENT + ROPE)
    values = jnp.clip(jax.random.normal(key, shape, jnp.float32), -4.0, 4.0) * 0.6
    return values.astype(jnp.bfloat16)


def block_scale(key, extent, pieces, low, high):
    gain, own = 1.0, jax.random.fold_in(key, 6)
    for axis_at, shards_of in pieces:
        steps = jnp.exp(jax.random.uniform(jax.random.fold_in(own, axis_at), (shards_of,), jnp.float32, low / len(pieces), high / len(pieces)))
        gain = gain * jnp.repeat(steps, extent[axis_at] // shards_of).reshape([-1 if axis == axis_at else 1 for axis in range(len(extent))])
    return gain


def centred(key, dims, spread, reach, cuts=(), kind=jnp.bfloat16):
    entries = spread * jax.random.normal(key, dims, jnp.float32)
    if cuts:
        entries = entries * block_scale(key, dims, cuts, -0.22, 0.18)
    return jnp.clip(entries, -reach, reach).astype(kind)


def setup_inputs(seed: int = 0) -> dict:
    seeds = jax.random.split(jax.random.key(seed), 5)
    return {
        "tokens": centred(seeds[0], (SEQ, D), 1.0, 6.0, ((0, 32), (1, 32))),
        "kv_down": centred(seeds[1], (D, LATENT + ROPE), D ** -0.5, 0.0625, ((0, 32),)),
        "norm_gain": jnp.clip(1.0 + 0.18 * jax.random.normal(seeds[2], (LATENT,), jnp.float32), 0.1, 1.9),
        "queries": draw_queries(jax.random.fold_in(seeds[4], 71), 0),
    }


epsilon = 1e-06
theta_base = 10000.0
score_scale = 192.0 ** (-0.5)

def finish(kv_raw, norm_gain, first_row):
    row_count = kv_raw.shape[0]
    latent_raw = kv_raw[:, :LATENT]
    squares = lax.optimization_barrier(jnp.mean(latent_raw * latent_raw, axis=1, keepdims=True))
    latent = latent_raw * lax.rsqrt(squares + epsilon) * norm_gain[None, :]
    half_size = ROPE // 2
    positions = (first_row + jnp.arange(row_count, dtype=jnp.int32)).astype(jnp.float32)
    frequency = theta_base ** (-jnp.arange(half_size, dtype=jnp.float32) / half_size)
    phases = positions[:, None] * frequency[None, :]
    cosine = jnp.cos(phases)
    sine = jnp.sin(phases)
    first_half = kv_raw[:, LATENT:LATENT + half_size]
    second_half = kv_raw[:, LATENT + half_size:]
    rotated = jnp.concatenate([first_half * cosine - second_half * sine, first_half * sine + second_half * cosine], axis=1)
    return jnp.concatenate([latent, rotated], axis=1).astype(jnp.bfloat16)

def attend(query_block, window, query_first, key_first):
    query_count = query_block.shape[0]
    key_count = window.shape[0]
    scores = jnp.einsum('thd,kd->thk', query_block.astype(jnp.float32), window.astype(jnp.float32)) * score_scale
    query_pos = query_first + jnp.arange(query_count, dtype=jnp.int32)
    key_pos = key_first + jnp.arange(key_count, dtype=jnp.int32)
    allowed = (key_pos[None, :] >= 0) & (key_pos[None, :] <= query_pos[:, None])
    scores = jnp.where(allowed[:, None, :], scores, jnp.float32(-1e+30))
    highest = lax.optimization_barrier(jnp.max(scores, axis=2, keepdims=True))
    expd = jnp.exp(scores - highest)
    weight_sum = lax.optimization_barrier(jnp.sum(expd, axis=2, keepdims=True))
    weights = expd.astype(jnp.bfloat16)
    values = window[:, :LATENT]
    mixed = jnp.einsum('thk,kd->thd', weights.astype(jnp.float32), values.astype(jnp.float32)) / weight_sum
    return mixed.astype(jnp.bfloat16)

def reference(tokens, kv_down, norm_gain, queries):
    kv_raw = jnp.dot(tokens, kv_down, preferred_element_type=jnp.float32)
    key_rows = finish(kv_raw, norm_gain, 0)
    padding = jnp.zeros((REACH * TOK_DEV, LATENT + ROPE), jnp.bfloat16)
    padded = jnp.concatenate([padding, key_rows], axis=0)

    def one_block(block_index):
        query_first = block_index * TOK_DEV
        query_block = lax.dynamic_slice_in_dim(queries, query_first, TOK_DEV, 0)
        window = lax.dynamic_slice_in_dim(padded, query_first, (REACH + 1) * TOK_DEV, 0)
        return attend(query_block, window, query_first, query_first - REACH * TOK_DEV)
    blocks = lax.map(one_block, jnp.arange(N_CTX, dtype=jnp.int32))
    return blocks.reshape(SEQ, HEADS, LATENT)
```

```python
import jax
import jax.numpy as jnp
from jax import lax
from jax.sharding import Mesh, PartitionSpec as P

LATENT = 512
ROPE = 64
REACH = 3

X, ZLO, Y, ZHI, CORE = 4, 8, 4, 4, 2
CTX = ("x", "zlo")
FSDP = ("y", "zhi", "core")

epsilon = 1e-06
theta_base = 10000.0
score_scale = 192.0 ** (-0.5)


def finish(kv_raw, norm_gain, positions):
    latent_raw = kv_raw[:, :LATENT]
    squares = jnp.mean(latent_raw * latent_raw, axis=1, keepdims=True)
    latent = latent_raw * lax.rsqrt(squares + epsilon) * norm_gain[None, :]
    half_size = ROPE // 2
    frequency = theta_base ** (-jnp.arange(half_size, dtype=jnp.float32) / half_size)
    phases = positions.astype(jnp.float32)[:, None] * frequency[None, :]
    cosine = jnp.cos(phases)
    sine = jnp.sin(phases)
    first_half = kv_raw[:, LATENT : LATENT + half_size]
    second_half = kv_raw[:, LATENT + half_size :]
    rotated = jnp.concatenate(
        [first_half * cosine - second_half * sine, first_half * sine + second_half * cosine], axis=1
    )
    return jnp.concatenate([latent, rotated], axis=1).astype(jnp.bfloat16)


def attend(query_block, window, query_pos, key_pos):
    scores = (
        jnp.einsum("thd,kd->thk", query_block, window, preferred_element_type=jnp.float32)
        * score_scale
    )
    allowed = (key_pos[None, :] >= 0) & (key_pos[None, :] <= query_pos[:, None])
    scores = jnp.where(allowed[:, None, :], scores, jnp.float32(-1e30))
    highest = jnp.max(scores, axis=2, keepdims=True)
    expd = jnp.exp(scores - highest)
    weight_sum = jnp.sum(expd, axis=2, keepdims=True)
    weights = expd.astype(jnp.bfloat16)
    mixed = (
        jnp.einsum("thk,kd->thd", weights, window[:, :LATENT], preferred_element_type=jnp.float32)
        / weight_sum
    )
    return mixed.astype(jnp.bfloat16)


def earlier_route(distance):
    route = []
    for x in range(X):
        for zlo in range(ZLO):
            for zhi in range(ZHI):
                sx, szlo, szhi = x, zlo - distance, zhi
                if szlo < 0:
                    sx, szlo, szhi = x - 1, szlo + ZLO, (zhi - 1) % ZHI
                if sx >= 0:
                    route.append(((sx * ZLO + szlo) * ZHI + szhi, (x * ZLO + zlo) * ZHI + zhi))
    return route


def per_device(tokens, kv_down, norm_gain, queries):
    row_count = tokens.shape[0]
    width = kv_down.shape[1]
    half = row_count // CORE
    piece = half // Y
    first_row = lax.axis_index(CTX) * row_count
    core = lax.axis_index("core")
    swap = [(0, 1), (1, 0)]

    partial_value = jnp.dot(tokens, kv_down, preferred_element_type=jnp.float32)
    sent = lax.dynamic_slice_in_dim(partial_value, (1 - core) * half, half, 0)
    kept = lax.dynamic_slice_in_dim(partial_value, core * half, half, 0)
    summed = kept + lax.ppermute(sent, "core", swap)
    summed = jnp.sum(lax.all_to_all(summed.reshape(Y, piece, width), "y", 0, 0), axis=0)
    sent = (summed * 64.0).astype(jnp.float16)
    summed = jnp.sum(lax.all_gather(sent, "zhi").astype(jnp.float32), axis=0) * (1.0 / 64.0)

    piece_first = first_row + core * half + lax.axis_index("y") * piece
    key_rows = finish(summed, norm_gain, piece_first + jnp.arange(piece, dtype=jnp.int32))
    blocks = [key_rows] + [
        lax.ppermute(key_rows, ("x", "zlo", "zhi"), earlier_route(d)) for d in range(1, REACH + 1)
    ]
    mine = lax.all_gather(jnp.concatenate(blocks, axis=0), "y", tiled=True)
    other = lax.ppermute(mine, "core", swap)
    window = jnp.concatenate([mine, other], axis=0)

    back = row_count * jnp.arange(REACH + 1, dtype=jnp.int32)
    half_pos = (
        first_row
        + piece * jnp.arange(Y, dtype=jnp.int32)[:, None, None]
        - back[None, :, None]
        + jnp.arange(piece, dtype=jnp.int32)[None, None, :]
    ).reshape(-1)
    key_pos = jnp.concatenate([half_pos + core * half, half_pos + (1 - core) * half])
    query_pos = first_row + jnp.arange(row_count, dtype=jnp.int32)
    return attend(queries, window, query_pos, key_pos)


def solution(mesh):
    fine = Mesh(mesh.devices.reshape(X, ZLO, Y, ZHI, CORE), CTX + FSDP)
    placed = (P(CTX, FSDP), P(FSDP, None), P(), P(CTX, FSDP, None))
    return jax.shard_map(
        per_device, mesh=fine, in_specs=placed, out_specs=P(CTX, FSDP, None), check_vma=False
    )
```

```python
import jax
import jax.numpy as jnp
from jax import lax
from jax.experimental import pallas as pl
from jax.experimental.layout import Layout, with_layout_constraint
from jax.experimental.pallas import tpu as pltpu
from jax.sharding import Mesh, PartitionSpec as P

LATENT = 512
ROPE = 64
REACH = 3

X, ZLO, Y, ZHI, CORE = 4, 8, 4, 4, 2
CTX = ("x", "zlo")
FSDP = ("y", "zhi", "core")

epsilon = 1e-06
theta_base = 10000.0
score_scale = 192.0 ** (-0.5)
LOG2_E = 1.4426950408889634
CHUNKS = 2
HEADS_DEV = 4


def finish(kv_raw, norm_gain, positions):
    latent_raw = kv_raw[:, :LATENT]
    squares = jnp.mean(latent_raw * latent_raw, axis=1, keepdims=True)
    latent = latent_raw * lax.rsqrt(squares + epsilon) * norm_gain[None, :]
    half_size = ROPE // 2
    frequency = theta_base ** (-jnp.arange(half_size, dtype=jnp.float32) / half_size)
    phases = positions.astype(jnp.float32)[:, None] * frequency[None, :]
    cosine = jnp.cos(phases)
    sine = jnp.sin(phases)
    first_half = kv_raw[:, LATENT : LATENT + half_size]
    second_half = kv_raw[:, LATENT + half_size :]
    rotated = jnp.concatenate(
        [first_half * cosine - second_half * sine, first_half * sine + second_half * cosine], axis=1
    )
    return jnp.concatenate([latent, rotated], axis=1).astype(jnp.bfloat16)


def attend_kernel(place_ref, q_ref, mine_ref, other_ref, out_ref):
    heads = out_ref.shape[1]
    rows = q_ref.shape[0] // CHUNKS
    keys = mine_ref.shape[0] * mine_ref.shape[2]
    first_row, core = place_ref[0], place_ref[1]
    piece = keys // (Y * (REACH + 1))
    block = piece * Y * CORE
    key = lax.broadcasted_iota(jnp.int32, (1, keys), 1)
    local = (
        key // (piece * (REACH + 1)) * piece
        + key % piece
        - key // piece % (REACH + 1) * block
    )
    bounds = []
    for half in (core, 1 - core):
        from_first = local + half * (piece * Y)
        bounds.append(jnp.where(from_first < -first_row, 1 << 20, from_first))
    halves = [
        jnp.concatenate([ref[y] for y in range(Y)], axis=1) for ref in (mine_ref, other_ref)
    ]

    def products(n):
        q = q_ref[n * rows : (n + 1) * rows, :]
        return [jnp.dot(q, half, preferred_element_type=jnp.float32) for half in halves]

    ahead = products(0)
    for n in range(CHUNKS):
        now = ahead
        if n + 1 < CHUNKS:
            ahead = products(n + 1)
        token = (lax.broadcasted_iota(jnp.int32, (rows, 1), 0) + n * rows) // heads
        now = [jnp.where(bound <= token, v, -1e30) for v, bound in zip(now, bounds)]
        highest = jnp.maximum(*[jnp.max(v, axis=1, keepdims=True) for v in now])
        expd = [jnp.exp2((v - highest) * (score_scale * LOG2_E)) for v in now]
        weight_sum = sum(jnp.sum(v, axis=1, keepdims=True) for v in expd)
        mixed = sum(
            lax.dot_general(
                v.astype(jnp.bfloat16),
                half[:LATENT],
                (((1,), (1,)), ((), ())),
                preferred_element_type=jnp.float32,
            )
            for v, half in zip(expd, halves)
        )
        mixed = mixed * (1.0 / weight_sum)
        out_ref[n * rows // heads : (n + 1) * rows // heads] = mixed.reshape(
            rows // heads, heads, LATENT
        ).astype(jnp.bfloat16)


def attend(query_rows, mine, other, first_row, core):
    whole = pl.BlockSpec(memory_space=pltpu.VMEM)
    rows = query_rows.shape[0]
    return pl.pallas_call(
        attend_kernel,
        out_shape=jax.ShapeDtypeStruct((rows // HEADS_DEV, HEADS_DEV, LATENT), jnp.bfloat16),
        in_specs=[pl.BlockSpec(memory_space=pltpu.SMEM), whole, whole, whole],
        out_specs=whole,
        name="attend",
        compiler_params=pltpu.CompilerParams(vmem_limit_bytes=40 << 20),
    )(
        jnp.stack([first_row, core]).astype(jnp.int32),
        query_rows,
        mine,
        other,
    )


def earlier_route(distance):
    route = []
    for x in range(X):
        for zlo in range(ZLO):
            for zhi in range(ZHI):
                sx, szlo, szhi = x, zlo - distance, zhi
                if szlo < 0:
                    sx, szlo, szhi = x - 1, szlo + ZLO, (zhi - 1) % ZHI
                if sx >= 0:
                    route.append(((sx * ZLO + szlo) * ZHI + szhi, (x * ZLO + zlo) * ZHI + zhi))
    return route


def per_device(tokens, kv_down, norm_gain, queries):
    row_count = tokens.shape[0]
    width = kv_down.shape[1]
    half = row_count // CORE
    piece = half // Y
    first_row = lax.axis_index(CTX) * row_count
    core = lax.axis_index("core")
    swap = [(0, 1), (1, 0)]

    partial_value = jnp.dot(tokens, kv_down, preferred_element_type=jnp.float32)
    partial_value = with_layout_constraint(partial_value, Layout((0, 1)))
    sent = lax.dynamic_slice_in_dim(partial_value, (1 - core) * half, half, 0)
    kept = lax.dynamic_slice_in_dim(partial_value, core * half, half, 0)
    summed = kept + lax.ppermute(sent, "core", swap)
    summed, queries = lax.optimization_barrier((summed, queries))
    summed = lax.all_to_all(summed.reshape(Y, piece, width), "y", 0, 0)
    summed, query_rows = lax.optimization_barrier((summed, queries.reshape(-1, width)))
    summed = jnp.sum(summed, axis=0)
    sent = (summed * 64.0).astype(jnp.float16)
    summed = jnp.sum(lax.all_gather(sent, "zhi").astype(jnp.float32), axis=0) * (1.0 / 64.0)

    piece_first = first_row + core * half + lax.axis_index("y") * piece
    key_rows = finish(summed, norm_gain, piece_first + jnp.arange(piece, dtype=jnp.int32))
    pair = jnp.concatenate(
        [key_rows, lax.ppermute(key_rows, ("x", "zlo", "zhi"), earlier_route(1))], axis=0
    )
    pieces = jnp.concatenate(
        [pair, lax.ppermute(pair, ("x", "zlo", "zhi"), earlier_route(2))], axis=0
    )
    keys = pieces.T
    mine = lax.all_to_all(jnp.broadcast_to(keys[None], (Y,) + keys.shape), "y", 0, 0)
    other = lax.ppermute(mine, "core", swap)
    return attend(query_rows, mine, other, first_row, core)


def solution(mesh):
    fine = Mesh(mesh.devices.reshape(X, ZLO, Y, ZHI, CORE), CTX + FSDP)
    placed = (P(CTX, FSDP), P(FSDP, None), P(), P(CTX, FSDP, None))
    return jax.shard_map(
        per_device, mesh=fine, in_specs=placed, out_specs=P(CTX, FSDP, None), check_vma=False
    )
```
